32 devices in a mesh: fsdp: 2 (over x), ctx: 4 (over z), tp: 4 (over y, core).
Axes of the slice: x: 2, y: 2, z: 4, core: 2. Of those that a mesh axis runs over, the one named last changes fastest.
Arguments:
- tokens: bfloat16 [2, 1024, 2560], P('fsdp', 'ctx'), may hold values from -6 to 6
- cotangent: bfloat16 [2, 1024, 2560], P('fsdp', 'ctx'), may hold values from -6 to 6
- block_order: int32 [2, 8], P('fsdp'), may hold values from 0 to 7, as said below
- latent_weight: bfloat16 [2560, 1056], P(('fsdp', 'ctx')), may hold values from -0.125 to 0.125
- query_up: bfloat16 [768, 3840], P(('fsdp', 'ctx'), 'tp'), may hold values from -0.21875 to 0.21875
- keyval_up: bfloat16 [256, 5120], P(('fsdp', 'ctx'), 'tp'), may hold values from -0.375 to 0.375
- output_weight: bfloat16 [2560, 2560], P(('fsdp', 'ctx'), 'tp'), may hold values from -2.5 to 2.5
- gate_weight: bfloat16 [2560, 6400], P(('fsdp', 'ctx'), 'tp'), may hold values from -0.125 to 0.125
- up_weight: bfloat16 [2560, 6400], P(('fsdp', 'ctx'), 'tp'), may hold values from -0.125 to 0.125
- down_weight: bfloat16 [2560, 6400], P(('fsdp', 'ctx'), 'tp'), may hold values from -0.4375 to 0.4375
- norm_gains: bfloat16 [6144], P(('fsdp', 'ctx')), may hold values from 0.25 to 2.5
- first_latent: float32 [2560, 1056], P(('fsdp', 'ctx')), may hold values from -1.9073486e-05 to 1.9073486e-05
- first_query: float32 [768, 3840], P(('fsdp', 'ctx'), 'tp'), may hold values from -1.9073486e-05 to 1.9073486e-05
- first_keyval: float32 [256, 5120], P(('fsdp', 'ctx'), 'tp'), may hold values from -1.9073486e-05 to 1.9073486e-05
- first_output: float32 [2560, 2560], P(('fsdp', 'ctx'), 'tp'), may hold values from -1.9073486e-06 to 1.9073486e-06
- first_gate: float32 [2560, 6400], P(('fsdp', 'ctx'), 'tp'), may hold values from -1.9073486e-05 to 1.9073486e-05
- first_up: float32 [2560, 6400], P(('fsdp', 'ctx'), 'tp'), may hold values from -1.9073486e-05 to 1.9073486e-05
- first_down: float32 [2560, 6400], P(('fsdp', 'ctx'), 'tp'), may hold values from -1.9073486e-05 to 1.9073486e-05
- first_gains: float32 [6144], P(('fsdp', 'ctx')), may hold values from -1.9073486e-05 to 1.9073486e-05
- second_latent: float32 [2560, 1056], P(('fsdp', 'ctx')), may hold values from 1.5955339e-13 to 4.7866017e-12
- second_query: float32 [768, 3840], P(('fsdp', 'ctx'), 'tp'), may hold values from 1.5955339e-13 to 4.7866017e-12
- second_keyval: float32 [256, 5120], P(('fsdp', 'ctx'), 'tp'), may hold values from 1.5955339e-13 to 4.7866017e-12
- second_output: float32 [2560, 2560], P(('fsdp', 'ctx'), 'tp'), may hold values from 1.5955339e-15 to 4.7866018e-14
- second_gate: float32 [2560, 6400], P(('fsdp', 'ctx'), 'tp'), may hold values from 1.5955339e-13 to 4.7866017e-12
- second_up: float32 [2560, 6400], P(('fsdp', 'ctx'), 'tp'), may hold values from 1.5955339e-13 to 4.7866017e-12
- second_down: float32 [2560, 6400], P(('fsdp', 'ctx'), 'tp'), may hold values from 1.595534e-14 to 4.786602e-13
- second_gains: float32 [6144], P(('fsdp', 'ctx')), may hold values from 1.5955339e-13 to 4.7866017e-12
Outputs:
- block_output: float32 [2, 1024, 2560], P('fsdp', ('ctx', 'tp'))
- input_grad: float32 [2, 1024, 2560], P('fsdp', ('ctx', 'tp'))
- latent_weight_gradient: float32 [2560, 1056], P(('fsdp', 'ctx'))
- grad_query: float32 [768, 3840], P(('fsdp', 'ctx'), 'tp')
- grad_keyval: float32 [256, 5120], P(('fsdp', 'ctx'), 'tp')
- output_weight_gradient: float32 [2560, 2560], P(('fsdp', 'ctx'), 'tp')
- gate_weight_gradient: float32 [2560, 6400], P(('fsdp', 'ctx'), 'tp')
- grad_up: float32 [2560, 6400], P(('fsdp', 'ctx'), 'tp')
- down_weight_gradient: float32 [2560, 6400], P(('fsdp', 'ctx'), 'tp')
- grad_gains: float32 [6144], P(('fsdp', 'ctx'))
- grad_norm: float32 [], replicated
- new_first_latent: float32 [2560, 1056], P(('fsdp', 'ctx'))
- new_first_query: float32 [768, 3840], P(('fsdp', 'ctx'), 'tp')
- new_first_keyval: float32 [256, 5120], P(('fsdp', 'ctx'), 'tp')
- new_first_output: float32 [2560, 2560], P(('fsdp', 'ctx'), 'tp')
- new_first_gate: float32 [2560, 6400], P(('fsdp', 'ctx'), 'tp')
- new_first_up: float32 [2560, 6400], P(('fsdp', 'ctx'), 'tp')
- new_first_down: float32 [2560, 6400], P(('fsdp', 'ctx'), 'tp')
- new_first_gains: float32 [6144], P(('fsdp', 'ctx'))
- new_second_latent: float32 [2560, 1056], P(('fsdp', 'ctx'))
- new_second_query: float32 [768, 3840], P(('fsdp', 'ctx'), 'tp')
- new_second_keyval: float32 [256, 5120], P(('fsdp', 'ctx'), 'tp')
- new_second_output: float32 [2560, 2560], P(('fsdp', 'ctx'), 'tp')
- new_second_gate: float32 [2560, 6400], P(('fsdp', 'ctx'), 'tp')
- new_second_up: float32 [2560, 6400], P(('fsdp', 'ctx'), 'tp')
- new_second_down: float32 [2560, 6400], P(('fsdp', 'ctx'), 'tp')
- new_second_gains: float32 [6144], P(('fsdp', 'ctx'))
- update_latent: float32 [2560, 1056], P(('fsdp', 'ctx'))
- update_query: float32 [768, 3840], P(('fsdp', 'ctx'), 'tp')
- update_keyval: float32 [256, 5120], P(('fsdp', 'ctx'), 'tp')
- update_output: float32 [2560, 2560], P(('fsdp', 'ctx'), 'tp')
- update_gate: float32 [2560, 6400], P(('fsdp', 'ctx'), 'tp')
- update_up: float32 [2560, 6400], P(('fsdp', 'ctx'), 'tp')
- update_down: float32 [2560, 6400], P(('fsdp', 'ctx'), 'tp')
- update_gains: float32 [6144], P(('fsdp', 'ctx'))
The draws below stay inside these ranges and needn't reach their ends.
Inputs may be any that keep to these rules, and one draw needn't show every extreme that they name: `block_order`: each row is a permutation of 0 to 7, and for every c the entries 2c and 2c + 1 of a row sum to 7.
All inputs are finite; a program needn't handle non-finite values.
Results may differ from the reference program's by a relative error of at most 0.039.
Values may be sent and summed in bfloat16 or wider, within the bound.
No kernel may reach another device: no remote copies, remote signals or barrier semaphores. Data moves between devices by JAX's collectives and lax.ppermute only.
A program may use at most 256 MiB of HBM per device.

```python
import math
import jax
import jax.numpy as jnp
from jax import lax

D = 2560
FF = 6400
HEADS = 40
NOPE = 64
ROPE = 32
VDIM = 64
QR = 768
KVR = 256
LEN = 1024
NSEQ = 2
LAT = 1056
GAINS = 6144
PARAMS = 62674944
N_CTX = 4


def draw_block_order(key, part):
    places = 2 * N_CTX

    def one_row(row_key):
        order_key, flip_key = jax.random.split(row_key)
        pair_order = jax.random.permutation(order_key, N_CTX)
        flip_bits = jax.random.randint(flip_key, (N_CTX,), 0, 2)
        leading = jnp.where(flip_bits == 1, places - 1 - pair_order, pair_order)
        return jnp.stack([leading, places - 1 - leading], axis=1).reshape(places)
    return jax.vmap(one_row)(jax.random.split(key, NSEQ)).astype(jnp.int32)


def draw_norm_gains(key, part):
    ramp = jnp.concatenate([jnp.linspace(0.0, 1.0, D, dtype=jnp.float32), jnp.linspace(0.0, 1.0, QR, dtype=jnp.float32), jnp.linspace(0.0, 1.0, KVR, dtype=jnp.float32), jnp.linspace(0.0, 1.0, D, dtype=jnp.float32)], axis=0)
    jitter = jax.random.uniform(jax.random.fold_in(key, 7), (GAINS,), jnp.float32, 0.85, 1.15)
    base = 0.5 + ramp
    return (base * jitter).astype(jnp.bfloat16)


def shard_levels(own_key, extent, shards, low, high):
    gain, own = 1.0, jax.random.fold_in(own_key, 6)
    for position, blocks in shards:
        steps = jnp.exp(jax.random.uniform(jax.random.fold_in(own, position), (blocks,), jnp.float32, low / len(shards), high / len(shards)))
        gain = gain * jnp.repeat(steps, extent[position] // blocks).reshape([-1 if axis == position else 1 for axis in range(len(extent))])
    return gain


def noise(own_key, dims, width, limit, shards=(), kind=jnp.bfloat16):
    drawn = width * jax.random.normal(own_key, dims, jnp.float32)
    if shards:
        drawn = drawn * shard_levels(own_key, dims, shards, -0.22, 0.18)
    return jnp.clip(drawn, -limit, limit).astype(kind)


def setup_inputs(seed: int = 0) -> dict:
    splits = jax.random.split(jax.random.key(seed), 28)
    tokens = noise(splits[0], (NSEQ, LEN, D), 1.0, 6.0, ((0, 2), (1, 4)))
    cotangent = noise(splits[1], (NSEQ, LEN, D), 1.0, 6.0, ((0, 2), (1, 4)))
    block_order = draw_block_order(jax.random.fold_in(splits[27], 71), 0)
    latent_weight = noise(splits[3], (D, LAT), D ** -0.5, 0.125, ((0, 8),))
    query_up = noise(splits[4], (QR, HEADS * (NOPE + ROPE)), QR ** -0.5, 0.21875, ((0, 8), (1, 4)))
    keyval_up = noise(splits[5], (KVR, HEADS * (NOPE + VDIM)), KVR ** -0.5, 0.375, ((0, 8), (1, 4)))
    output_weight = noise(splits[6], (D, HEADS * VDIM), (max(HEADS * VDIM // 512, 1)) ** -0.5, 2.5, ((0, 8), (1, 4)))
    gate_weight = noise(splits[7], (D, FF), D ** -0.5, 0.125, ((0, 8), (1, 4)))
    up_weight = noise(splits[8], (D, FF), D ** -0.5, 0.125, ((0, 8), (1, 4)))
    down_weight = noise(splits[9], (D, FF), (max(FF // 32, 1)) ** -0.5, 0.4375, ((0, 8), (1, 4)))
    norm_gains = draw_norm_gains(jax.random.fold_in(splits[27], 71), 0)
    first_latent = noise(splits[11], (D, LAT), (0.01 * PARAMS ** -0.5), 1.9073486328125e-05, ((0, 8),), jnp.float32)
    first_query = noise(splits[12], (QR, HEADS * (NOPE + ROPE)), (0.01 * PARAMS ** -0.5), 1.9073486328125e-05, ((0, 8), (1, 4)), jnp.float32)
    first_keyval = noise(splits[13], (KVR, HEADS * (NOPE + VDIM)), (0.01 * PARAMS ** -0.5), 1.9073486328125e-05, ((0, 8), (1, 4)), jnp.float32)
    first_output = noise(splits[14], (D, HEADS * VDIM), (0.001 * PARAMS ** -0.5), 1.9073486328125e-06, ((0, 8), (1, 4)), jnp.float32)
    first_gate = noise(splits[15], (D, FF), (0.01 * PARAMS ** -0.5), 1.9073486328125e-05, ((0, 8), (1, 4)), jnp.float32)
    first_up = noise(splits[16], (D, FF), (0.01 * PARAMS ** -0.5), 1.9073486328125e-05, ((0, 8), (1, 4)), jnp.float32)
    first_down = noise(splits[17], (D, FF), (0.01 * PARAMS ** -0.5), 1.9073486328125e-05, ((0, 8), (1, 4)), jnp.float32)
    first_gains = noise(splits[18], (GAINS,), (0.01 * PARAMS ** -0.5), 1.9073486328125e-05, ((0, 8),), jnp.float32)
    second_latent = jnp.clip(jnp.exp(math.log(4.786601670581092e-12) - 3.4011974 * jax.random.uniform(splits[19], (D, LAT), jnp.float32) ** shard_levels(splits[19], (D, LAT), ((0, 8),), -0.2, 0.2)), 1.5955338721236612e-13, 4.786601670581092e-12)
    second_query = jnp.clip(jnp.exp(math.log(4.786601670581092e-12) - 3.4011974 * jax.random.uniform(splits[20], (QR, HEADS * (NOPE + ROPE)), jnp.float32) ** shard_levels(splits[20], (QR, HEADS * (NOPE + ROPE)), ((0, 8), (1, 4)), -0.2, 0.2)), 1.5955338721236612e-13, 4.786601670581092e-12)
    second_keyval = jnp.clip(jnp.exp(math.log(4.786601670581092e-12) - 3.4011974 * jax.random.uniform(splits[21], (KVR, HEADS * (NOPE + VDIM)), jnp.float32) ** shard_levels(splits[21], (KVR, HEADS * (NOPE + VDIM)), ((0, 8), (1, 4)), -0.2, 0.2)), 1.5955338721236612e-13, 4.786601670581092e-12)
    second_output = jnp.clip(jnp.exp(math.log(4.786601819658891e-14) - 3.4011974 * jax.random.uniform(splits[22], (D, HEADS * VDIM), jnp.float32) ** shard_levels(splits[22], (D, HEADS * VDIM), ((0, 8), (1, 4)), -0.2, 0.2)), 1.595533939886297e-15, 4.786601819658891e-14)
    second_gate = jnp.clip(jnp.exp(math.log(4.786601670581092e-12) - 3.4011974 * jax.random.uniform(splits[23], (D, FF), jnp.float32) ** shard_levels(splits[23], (D, FF), ((0, 8), (1, 4)), -0.2, 0.2)), 1.5955338721236612e-13, 4.786601670581092e-12)
    second_up = jnp.clip(jnp.exp(math.log(4.786601670581092e-12) - 3.4011974 * jax.random.uniform(splits[24], (D, FF), jnp.float32) ** shard_levels(splits[24], (D, FF), ((0, 8), (1, 4)), -0.2, 0.2)), 1.5955338721236612e-13, 4.786601670581092e-12)
    second_down = jnp.clip(jnp.exp(math.log(4.786601887421527e-13) - 3.4011974 * jax.random.uniform(splits[25], (D, FF), jnp.float32) ** shard_levels(splits[25], (D, FF), ((0, 8), (1, 4)), -0.2, 0.2)), 1.595533939886297e-14, 4.786601887421527e-13)
    second_gains = jnp.clip(jnp.exp(math.log(4.786601670581092e-12) - 3.4011974 * jax.random.uniform(splits[26], (GAINS,), jnp.float32) ** shard_levels(splits[26], (GAINS,), ((0, 8),), -0.2, 0.2)), 1.5955338721236612e-13, 4.786601670581092e-12)
    return dict(tokens=tokens, cotangent=cotangent, block_order=block_order, latent_weight=latent_weight, query_up=query_up, keyval_up=keyval_up, output_weight=output_weight, gate_weight=gate_weight, up_weight=up_weight, down_weight=down_weight, norm_gains=norm_gains, first_latent=first_latent, first_query=first_query, first_keyval=first_keyval, first_output=first_output, first_gate=first_gate, first_up=first_up, first_down=first_down, first_gains=first_gains, second_latent=second_latent, second_query=second_query, second_keyval=second_keyval, second_output=second_output, second_gate=second_gate, second_up=second_up, second_down=second_down, second_gains=second_gains)


@jax.custom_vjp
def low(v):
    return lax.optimization_barrier(v.astype(jnp.bfloat16)).astype(jnp.float32)

@jax.custom_vjp
def low_back(v):
    return v

def low_keep(v):
    return (low(v), None)

def low_pass(kept, grad):
    return (grad,)

def back_keep(v):
    return (v, None)

def back_low(kept, grad):
    return (low(grad),)
low.defvjp(low_keep, low_pass)
low_back.defvjp(back_keep, back_low)
residual_scale = 1.4 / math.sqrt(62.0)
norm_eps = 1e-05
clip_level = 0.01
beta_first = 0.5
beta_second = 0.5
learn_rate = 0.05
decay_rate = 0.1
adam_eps = 1e-08
step_count = 3.0

def dot_high(left, right):
    return jnp.dot(left, right, precision=lax.Precision.HIGHEST)

def einsum_high(form, left, right):
    return jnp.einsum(form, left, right, precision=lax.Precision.HIGHEST)

def norm_apply(values, norm_gain):
    inverse = lax.rsqrt(lax.optimization_barrier(jnp.mean(values * values, axis=-1, keepdims=True)) + norm_eps)
    return values * inverse * norm_gain

def rope_tables(positions):
    half_size = ROPE // 2
    frequency = jnp.exp(-math.log(10000.0) * (2.0 * jnp.arange(half_size, dtype=jnp.float32) / ROPE))
    angles = positions[..., None] * frequency
    return (jnp.cos(angles), jnp.sin(angles))

def rotate(values, cosine_table, sine_table):
    half_size = values.shape[-1] // 2
    front_half = values[..., :half_size]
    back_half = values[..., half_size:]
    return jnp.concatenate([front_half * cosine_table - back_half * sine_table, back_half * cosine_table + front_half * sine_table], axis=-1)

def attention(queries, key_nope, key_rope, value_rows, positions):
    row_block = math.gcd(LEN, 512)
    block_count = LEN // row_block
    query_blocks = queries.reshape(block_count, row_block, HEADS, NOPE + ROPE)
    place_blocks = positions.reshape(block_count, row_block)
    score_scale = 1.0 / math.sqrt(NOPE + ROPE)

    def one_block(packed):
        query_rows, query_place = packed
        raw_scores = einsum_high('ihd,jhd->hij', query_rows[..., :NOPE], key_nope)
        raw_scores = raw_scores + einsum_high('ihd,jd->hij', query_rows[..., NOPE:], key_rope)
        visible = positions[None, None, :] <= query_place[None, :, None]
        scores = low_back(jnp.where(visible, raw_scores * score_scale, -1e+30))
        row_max = lax.optimization_barrier(jnp.max(scores, axis=-1, keepdims=True))
        exponent = jnp.exp(scores - row_max)
        attend_probs = exponent / lax.optimization_barrier(jnp.sum(exponent, axis=-1, keepdims=True))
        return einsum_high('hij,jhd->ihd', low(attend_probs), value_rows)
    outcome = lax.map(jax.checkpoint(one_block), (query_blocks, place_blocks))
    return outcome.reshape(LEN, HEADS * VDIM)

def sequence_forward(params, inputs, positions):
    latent_weight, query_up, keyval_up, output_weight, gate_weight, up_weight, down_weight, norm_gains = params
    attend_gain = norm_gains[:D]
    query_gain = norm_gains[D:D + QR]
    keyval_gain = norm_gains[D + QR:D + QR + KVR]
    feed_gain = norm_gains[D + QR + KVR:]
    cosine_table, sine_table = rope_tables(positions)
    normalized_input = low(norm_apply(inputs, attend_gain))
    latent_projection = low_back(dot_high(normalized_input, latent_weight))
    query_latent = low(norm_apply(latent_projection[:, :QR], query_gain))
    keyval_latent = low(norm_apply(latent_projection[:, QR:QR + KVR], keyval_gain))
    key_rope = low(rotate(latent_projection[:, QR + KVR:], cosine_table, sine_table))
    query_pre = low_back(dot_high(query_latent, query_up)).reshape(LEN, HEADS, NOPE + ROPE)
    queries = low(jnp.concatenate([query_pre[..., :NOPE], rotate(query_pre[..., NOPE:], cosine_table[:, None, :], sine_table[:, None, :])], axis=-1))
    keyval = low(low_back(dot_high(keyval_latent, keyval_up))).reshape(LEN, HEADS, NOPE + VDIM)
    attention_result = low(low_back(attention(queries, keyval[..., :NOPE], key_rope, keyval[..., NOPE:], positions)))
    branch = low_back(dot_high(attention_result, output_weight.T))
    hidden = inputs + residual_scale * branch
    normalized_feed_input = low(norm_apply(hidden, feed_gain))
    gate_activation = low_back(dot_high(normalized_feed_input, gate_weight))
    upward_projection = low_back(dot_high(normalized_feed_input, up_weight))
    activation_rows = low(gate_activation * jax.nn.sigmoid(gate_activation) * upward_projection)
    feed_out = low_back(dot_high(activation_rows, down_weight.T))
    return hidden + residual_scale * feed_out

def adam_step(weight, gradient, first_old, second_old, factor, decayed):
    clipped = gradient * factor
    first_new = beta_first * first_old + (1.0 - beta_first) * clipped
    second_new = beta_second * second_old + (1.0 - beta_second) * clipped * clipped
    first_hat = first_new / (1.0 - beta_first ** step_count)
    second_hat = second_new / (1.0 - beta_second ** step_count)
    change = first_hat / (jnp.sqrt(second_hat) + adam_eps)
    if decayed:
        change = change + decay_rate * weight
    return (first_new, second_new, -learn_rate * change)

def reference(tokens, cotangent, block_order, latent_weight, query_up, keyval_up, output_weight, gate_weight, up_weight, down_weight, norm_gains, first_latent, first_query, first_keyval, first_output, first_gate, first_up, first_down, first_gains, second_latent, second_query, second_keyval, second_output, second_gate, second_up, second_down, second_gains):
    block_length = LEN // (2 * N_CTX)
    offsets = jnp.arange(block_length, dtype=jnp.int32)
    positions = (block_order.astype(jnp.int32)[:, :, None] * block_length + offsets[None, None, :]).reshape(NSEQ, LEN)
    positions = positions.astype(jnp.float32)
    weights = tuple((weight_item.astype(jnp.float32) for weight_item in (latent_weight, query_up, keyval_up, output_weight, gate_weight, up_weight, down_weight, norm_gains)))
    inputs = tokens.astype(jnp.float32)

    def forward(params, values):

        def one_sequence(packed):
            return sequence_forward(params, packed[0], packed[1])
        return lax.map(jax.checkpoint(one_sequence), (values, positions))
    outputs, pullback = jax.vjp(forward, weights, inputs)
    weight_sums, input_sum = pullback(cotangent.astype(jnp.float32))
    token_total = NSEQ * LEN
    grads = tuple((gradient / token_total for gradient in weight_sums))
    total_square = jnp.sum(grads[0] * grads[0])
    for gradient in grads[1:]:
        total_square = total_square + jnp.sum(gradient * gradient)
    grad_norm = jnp.sqrt(total_square)
    factor = clip_level / jnp.maximum(grad_norm, clip_level)
    firsts = (first_latent, first_query, first_keyval, first_output, first_gate, first_up, first_down, first_gains)
    seconds = (second_latent, second_query, second_keyval, second_output, second_gate, second_up, second_down, second_gains)
    new_first = []
    new_second = []
    changes = []
    for index_item in range(8):
        first_new, second_new, change = adam_step(weights[index_item], grads[index_item], firsts[index_item], seconds[index_item], factor, index_item < 7)
        new_first.append(first_new)
        new_second.append(second_new)
        changes.append(change)
    return (outputs, input_sum, grads[0], grads[1], grads[2], grads[3], grads[4], grads[5], grads[6], grads[7], grad_norm, new_first[0], new_first[1], new_first[2], new_first[3], new_first[4], new_first[5], new_first[6], new_first[7], new_second[0], new_second[1], new_second[2], new_second[3], new_second[4], new_second[5], new_second[6], new_second[7], changes[0], changes[1], changes[2], changes[3], changes[4], changes[5], changes[6], changes[7])
```

```python
import math

import jax
import jax.numpy as jnp
from jax import lax
from jax.sharding import PartitionSpec as P

HEADS = 40
NOPE = 64
ROPE = 32
VDIM = 64
QR = 768
KVR = 256

FSDP = "fsdp"
CTX = "ctx"
TP = "tp"
SPLIT = P((FSDP, CTX), TP)
ROWS = P((FSDP, CTX), None)
GAIN = P((FSDP, CTX))


residual_scale = 1.4 / math.sqrt(62.0)
norm_eps = 1e-05
clip_level = 0.01
beta_first = 0.5
beta_second = 0.5
learn_rate = 0.05
decay_rate = 0.1
adam_eps = 1e-08
step_count = 3.0


def contraction_product(form, left, right):
    return jnp.einsum(form, left, right, preferred_element_type=jnp.float32)


def norm_apply(values, norm_gain):
    inverse = lax.rsqrt(jnp.mean(values * values, axis=-1, keepdims=True) + norm_eps)
    return values * inverse * norm_gain


def norm_back(values, norm_gain, incoming):
    inverse = lax.rsqrt(jnp.mean(values * values, axis=-1, keepdims=True) + norm_eps)
    unit_rows = values * inverse
    scaled = incoming * norm_gain
    value_grad = inverse * (
        scaled - unit_rows * jnp.mean(unit_rows * scaled, axis=-1, keepdims=True)
    )
    return (value_grad, incoming * unit_rows)


def rope_tables(positions):
    half_size = ROPE // 2
    frequency = jnp.exp(
        -math.log(10000.0) * (2.0 * jnp.arange(half_size, dtype=jnp.float32) / ROPE)
    )
    angles = positions[..., None] * frequency
    return (jnp.cos(angles), jnp.sin(angles))


def rotate(values, cosine_table, sine_table):
    half_size = values.shape[-1] // 2
    front_half = values[..., :half_size]
    back_half = values[..., half_size:]
    return jnp.concatenate(
        [
            front_half * cosine_table - back_half * sine_table,
            back_half * cosine_table + front_half * sine_table,
        ],
        axis=-1,
    )


def rotate_back(values, cosine_table, sine_table):
    half_size = values.shape[-1] // 2
    front_half = values[..., :half_size]
    back_half = values[..., half_size:]
    return jnp.concatenate(
        [
            front_half * cosine_table + back_half * sine_table,
            back_half * cosine_table - front_half * sine_table,
        ],
        axis=-1,
    )


def adam_step(weight, gradient, first_old, second_old, factor, decayed):
    clipped = gradient * factor
    first_new = beta_first * first_old + (1.0 - beta_first) * clipped
    second_new = beta_second * second_old + (1.0 - beta_second) * clipped * clipped
    first_hat = first_new / (1.0 - beta_first**step_count)
    second_hat = second_new / (1.0 - beta_second**step_count)
    change = first_hat / (jnp.sqrt(second_hat) + adam_eps)
    if decayed:
        change = change + decay_rate * weight.astype(jnp.float32)
    return (first_new, second_new, -learn_rate * change)


def body_gathered(
    tokens,
    cotangent,
    block_order,
    latent_weight,
    query_up,
    keyval_up,
    output_weight,
    gate_weight,
    up_weight,
    down_weight,
    norm_gains,
    first_latent,
    first_query,
    first_keyval,
    first_output,
    first_gate,
    first_up,
    first_down,
    first_gains,
    second_latent,
    second_query,
    second_keyval,
    second_output,
    second_gate,
    second_up,
    second_down,
    second_gains,
):
    context_count = lax.axis_size(CTX)
    tensor_count = lax.axis_size(TP)
    shard_count = lax.axis_size(FSDP)
    context_place = lax.axis_index(CTX)
    tensor_place = lax.axis_index(TP)
    sequences, local_length, width = tokens.shape
    full_length = local_length * context_count
    share_length = local_length // tensor_count
    share_start = tensor_place * share_length
    local_heads = HEADS // tensor_count
    block_length = full_length // (2 * context_count)
    token_total = sequences * full_length * shard_count
    owner_count = shard_count * context_count
    row_piece = width // (owner_count * tensor_count)
    score_scale = 1.0 / math.sqrt(NOPE + ROPE)
    gathered = (
        lax.all_gather(latent_weight, (FSDP, CTX), axis=0, tiled=True),
        lax.all_gather(query_up, (FSDP, CTX), axis=0, tiled=True),
        lax.all_gather(keyval_up, (FSDP, CTX), axis=0, tiled=True),
        lax.all_gather(output_weight, (FSDP, CTX), axis=0, tiled=True),
        lax.all_gather(gate_weight, (FSDP, CTX), axis=0, tiled=True),
        lax.all_gather(up_weight, (FSDP, CTX), axis=0, tiled=True),
        lax.all_gather(down_weight, (FSDP, CTX), axis=0, tiled=True),
        lax.all_gather(norm_gains, (FSDP, CTX), axis=0, tiled=True),
    )
    (
        latent_weight_complete,
        query_full,
        keyval_full,
        output_weight_complete,
        gate_weight_complete,
        up_weight_complete,
        down_weight_complete,
        gain_full,
    ) = gathered
    gain_float = gain_full.astype(jnp.float32)
    attend_gain = gain_float[:width]
    query_gain = gain_float[width : width + QR]
    keyval_gain = gain_float[width + QR : width + QR + KVR]
    feed_gain = gain_float[width + QR + KVR :]
    offsets = jnp.arange(block_length, dtype=jnp.int32)
    position_all = (block_order[:, :, None] * block_length + offsets[None, None, :]).reshape(
        sequences, full_length
    )
    position_all = position_all.astype(jnp.float32)
    position_here = lax.dynamic_slice_in_dim(
        position_all, context_place * local_length, local_length, 1
    )
    cosine_here, sine_here = rope_tables(position_here)
    inputs = tokens.astype(jnp.float32)
    normalized_input = norm_apply(inputs, attend_gain).astype(jnp.bfloat16)
    latent_projection = contraction_product("kai,it->kat", normalized_input, latent_weight_complete)
    query_latent = norm_apply(latent_projection[..., :QR], query_gain).astype(jnp.bfloat16)
    keyval_latent = norm_apply(latent_projection[..., QR : QR + KVR], keyval_gain).astype(
        jnp.bfloat16
    )
    key_rope = rotate(latent_projection[..., QR + KVR :], cosine_here, sine_here).astype(
        jnp.bfloat16
    )
    query_pre = contraction_product("slr,re->sle", query_latent, query_full).reshape(
        sequences, local_length, local_heads, NOPE + ROPE
    )
    queries = jnp.concatenate(
        [
            query_pre[..., :NOPE],
            rotate(query_pre[..., NOPE:], cosine_here[:, :, None, :], sine_here[:, :, None, :]),
        ],
        axis=-1,
    ).astype(jnp.bfloat16)
    keyval = contraction_product("slr,re->sle", keyval_latent, keyval_full).astype(jnp.bfloat16)
    keyval_all, rope_all = (
        lax.all_gather(keyval, CTX, axis=1, tiled=True),
        lax.all_gather(key_rope, CTX, axis=1, tiled=True),
    )
    keyval_heads = keyval_all.reshape(sequences, full_length, local_heads, NOPE + VDIM)
    key_nope = keyval_heads[..., :NOPE]
    value_rows = keyval_heads[..., NOPE:]
    visible = position_all[:, None, None, :] <= position_here[:, None, :, None]

    def score_table():
        raw_scores = contraction_product("sihd,sjhd->shij", queries[..., :NOPE], key_nope)
        raw_scores = raw_scores + contraction_product(
            "sihd,sjd->shij", queries[..., NOPE:], rope_all
        )
        return jnp.where(visible, raw_scores * score_scale, -1e30)

    scores = score_table()
    row_max = jnp.max(scores, axis=-1, keepdims=True)
    exponent = jnp.exp(scores - row_max)
    row_sum = jnp.sum(exponent, axis=-1, keepdims=True)
    probs_low = (exponent / row_sum).astype(jnp.bfloat16)
    attention_result = contraction_product("shij,sjhd->sihd", probs_low, value_rows)
    attention_result = attention_result.reshape(sequences, local_length, local_heads * VDIM).astype(
        jnp.bfloat16
    )
    branch_portion = contraction_product("nyz,hz->nyh", attention_result, output_weight_complete)
    branch = lax.psum(branch_portion, TP)
    hidden = inputs + residual_scale * branch
    normalized_feed_input = norm_apply(hidden, feed_gain).astype(jnp.bfloat16)
    gate_activation = contraction_product(
        "ewt,tu->ewu", normalized_feed_input, gate_weight_complete
    )
    upward_projection = contraction_product(
        "ewt,tu->ewu", normalized_feed_input, up_weight_complete
    )
    sigmoid_gate = jax.nn.sigmoid(gate_activation)
    silu_gate = gate_activation * sigmoid_gate
    activation_rows = (silu_gate * upward_projection).astype(jnp.bfloat16)
    feed_portion = contraction_product("umw,vw->umv", activation_rows, down_weight_complete)
    feed_total = lax.psum(feed_portion.astype(jnp.bfloat16), TP).astype(jnp.float32)
    output_rows = lax.dynamic_slice_in_dim(
        hidden + residual_scale * feed_total, share_start, share_length, 1
    )
    incoming = cotangent.astype(jnp.float32)
    feed_gradient_start = (residual_scale * incoming).astype(jnp.bfloat16)
    activation_gradient = contraction_product(
        "ewt,tu->ewu", feed_gradient_start, down_weight_complete
    )
    gate_gradient_rows = (
        activation_gradient
        * upward_projection
        * sigmoid_gate
        * (1.0 + gate_activation * (1.0 - sigmoid_gate))
    ).astype(jnp.bfloat16)
    upward_gradient_rows = (activation_gradient * silu_gate).astype(jnp.bfloat16)
    down_weight_gradient = contraction_product("ubn,ubt->nt", feed_gradient_start, activation_rows)
    gate_weight_gradient = contraction_product(
        "ubn,ubt->nt", normalized_feed_input, gate_gradient_rows
    )
    upward_weight_gradient = contraction_product(
        "ubn,ubt->nt", normalized_feed_input, upward_gradient_rows
    )
    normalized_gradient_portion = contraction_product(
        "umw,vw->umv", gate_gradient_rows, gate_weight_complete
    ) + contraction_product("umw,vw->umv", upward_gradient_rows, up_weight_complete)
    normed_grad = lax.psum(normalized_gradient_portion, TP)
    hidden_back, gain_rows = norm_back(hidden, feed_gain, normed_grad)
    hidden_grad = incoming + hidden_back
    feed_gain_part = jnp.sum(
        lax.dynamic_slice_in_dim(gain_rows, share_start, share_length, 1), axis=(0, 1)
    )
    branch_gradient_part = (residual_scale * hidden_grad).astype(jnp.bfloat16)
    hidden_grad_share = lax.dynamic_slice_in_dim(hidden_grad, share_start, share_length, 1)
    output_weight_gradient = contraction_product(
        "zxg,zxn->gn", branch_gradient_part, attention_result
    )
    attention_result_gradient = contraction_product(
        "rnq,qk->rnk", branch_gradient_part, output_weight_complete
    ).astype(jnp.bfloat16)
    attention_result_gradient = attention_result_gradient.reshape(
        sequences, local_length, local_heads, VDIM
    )
    scores = score_table()
    attend_probs = jnp.exp(scores - row_max) / row_sum
    probs_low = attend_probs.astype(jnp.bfloat16)
    prob_grad = contraction_product("sihd,sjhd->shij", attention_result_gradient, value_rows)
    score_grad = (
        attend_probs * (prob_grad - jnp.sum(attend_probs * prob_grad, axis=-1, keepdims=True))
    ).astype(jnp.bfloat16)
    query_grad = (
        jnp.concatenate(
            [
                contraction_product("shij,sjhd->sihd", score_grad, key_nope),
                contraction_product("shij,sjd->sihd", score_grad, rope_all),
            ],
            axis=-1,
        )
        * score_scale
    )
    key_nope_grad = (
        contraction_product("shij,sihd->sjhd", score_grad, queries[..., :NOPE]) * score_scale
    )
    value_grad = contraction_product("shij,sihd->sjhd", probs_low, attention_result_gradient)
    rope_grad_all = (
        contraction_product("shij,sihd->sjd", score_grad, queries[..., NOPE:]) * score_scale
    )
    keyval_grad_all = jnp.concatenate([key_nope_grad, value_grad], axis=-1)
    keyval_grad_all = keyval_grad_all.reshape(sequences, full_length, local_heads * (NOPE + VDIM))
    keyval_grad, rope_grad = (
        lax.psum_scatter(
            keyval_grad_all.astype(jnp.bfloat16), CTX, scatter_dimension=1, tiled=True
        ).astype(jnp.float32),
        lax.psum_scatter(
            rope_grad_all.astype(jnp.bfloat16), CTX, scatter_dimension=1, tiled=True
        ).astype(jnp.float32),
    )
    query_pre_grad = jnp.concatenate(
        [
            query_grad[..., :NOPE],
            rotate_back(
                query_grad[..., NOPE:], cosine_here[:, :, None, :], sine_here[:, :, None, :]
            ),
        ],
        axis=-1,
    )
    query_pre_grad = query_pre_grad.reshape(
        sequences, local_length, local_heads * (NOPE + ROPE)
    ).astype(jnp.bfloat16)
    grad_query = contraction_product("slr,sle->re", query_latent, query_pre_grad)
    keyval_grad_low = keyval_grad.astype(jnp.bfloat16)
    grad_keyval = contraction_product("slr,sle->re", keyval_latent, keyval_grad_low)
    latent_grad_part = jnp.concatenate(
        [
            contraction_product("sle,re->slr", query_pre_grad, query_full),
            contraction_product("sle,re->slr", keyval_grad_low, keyval_full),
            rope_grad,
        ],
        axis=-1,
    )
    latent_grad_sum, feed_gain_grad = (
        lax.psum(latent_grad_part.astype(jnp.bfloat16), TP).astype(jnp.float32),
        lax.psum(feed_gain_part.astype(jnp.bfloat16), TP).astype(jnp.float32),
    )
    query_lat_grad, query_gain_rows = norm_back(
        latent_projection[..., :QR], query_gain, latent_grad_sum[..., :QR]
    )
    keyval_lat_grad, keyval_gain_rows = norm_back(
        latent_projection[..., QR : QR + KVR], keyval_gain, latent_grad_sum[..., QR : QR + KVR]
    )
    rope_lat_grad = rotate_back(latent_grad_sum[..., QR + KVR :], cosine_here, sine_here)
    latent_gradient_rows = jnp.concatenate(
        [query_lat_grad, keyval_lat_grad, rope_lat_grad], axis=-1
    ).astype(jnp.bfloat16)
    normed_split = normalized_input.reshape(
        sequences, local_length, owner_count, tensor_count, row_piece
    )
    normed_pick = lax.dynamic_index_in_dim(normed_split, tensor_place, 3, False)
    normed_pick = normed_pick.reshape(sequences, local_length, owner_count * row_piece)
    latent_weight_gradient = contraction_product("pjo,pjm->om", normed_pick, latent_gradient_rows)
    normalized_attention_gradient = contraction_product(
        "ycj,kj->yck", latent_gradient_rows, latent_weight_complete
    )
    input_back, attend_gain_rows = norm_back(inputs, attend_gain, normalized_attention_gradient)
    input_grad = hidden_grad_share + lax.dynamic_slice_in_dim(
        input_back, share_start, share_length, 1
    )
    gain_grad_full = jnp.concatenate(
        [
            jnp.sum(attend_gain_rows, axis=(0, 1)),
            jnp.sum(query_gain_rows, axis=(0, 1)),
            jnp.sum(keyval_gain_rows, axis=(0, 1)),
            feed_gain_grad,
        ],
        axis=0,
    )
    summed = (
        lax.psum_scatter(
            latent_weight_gradient.astype(jnp.bfloat16),
            (FSDP, CTX),
            scatter_dimension=0,
            tiled=True,
        ).astype(jnp.float32),
        lax.psum_scatter(
            grad_query.astype(jnp.bfloat16), (FSDP, CTX), scatter_dimension=0, tiled=True
        ).astype(jnp.float32),
        lax.psum_scatter(
            grad_keyval.astype(jnp.bfloat16), (FSDP, CTX), scatter_dimension=0, tiled=True
        ).astype(jnp.float32),
        lax.psum_scatter(
            output_weight_gradient.astype(jnp.bfloat16),
            (FSDP, CTX),
            scatter_dimension=0,
            tiled=True,
        ).astype(jnp.float32),
        lax.psum_scatter(
            gate_weight_gradient.astype(jnp.bfloat16),
            (FSDP, CTX),
            scatter_dimension=0,
            tiled=True,
        ).astype(jnp.float32),
        lax.psum_scatter(
            upward_weight_gradient.astype(jnp.bfloat16),
            (FSDP, CTX),
            scatter_dimension=0,
            tiled=True,
        ).astype(jnp.float32),
        lax.psum_scatter(
            down_weight_gradient.astype(jnp.bfloat16),
            (FSDP, CTX),
            scatter_dimension=0,
            tiled=True,
        ).astype(jnp.float32),
        lax.psum_scatter(
            gain_grad_full.astype(jnp.bfloat16), (FSDP, CTX), scatter_dimension=0, tiled=True
        ).astype(jnp.float32),
    )
    latent_owned = lax.all_gather(summed[0].astype(jnp.bfloat16), TP, axis=0, tiled=True).astype(
        jnp.float32
    )
    shards = tuple((shard_grad / token_total for shard_grad in (latent_owned,) + tuple(summed[1:])))
    lead_flag = (tensor_place == 0).astype(jnp.float32)
    local_square = lead_flag * (jnp.sum(shards[0] * shards[0]) + jnp.sum(shards[7] * shards[7]))
    for shard_grad in shards[1:7]:
        local_square = local_square + jnp.sum(shard_grad * shard_grad)
    total_square = lax.psum(local_square, (FSDP, CTX, TP))
    grad_norm = jnp.sqrt(total_square)
    factor = clip_level / jnp.maximum(grad_norm, clip_level)
    weights_local = (
        latent_weight,
        query_up,
        keyval_up,
        output_weight,
        gate_weight,
        up_weight,
        down_weight,
        norm_gains,
    )
    firsts = (
        first_latent,
        first_query,
        first_keyval,
        first_output,
        first_gate,
        first_up,
        first_down,
        first_gains,
    )
    seconds = (
        second_latent,
        second_query,
        second_keyval,
        second_output,
        second_gate,
        second_up,
        second_down,
        second_gains,
    )
    new_first = []
    new_second = []
    changes = []
    for index_item in range(8):
        first_new, second_new, change = adam_step(
            weights_local[index_item],
            shards[index_item],
            firsts[index_item],
            seconds[index_item],
            factor,
            index_item < 7,
        )
        new_first.append(first_new)
        new_second.append(second_new)
        changes.append(change)
    return (
        (output_rows, input_grad)
        + shards
        + (grad_norm,)
        + tuple(new_first)
        + tuple(new_second)
        + tuple(changes)
    )


def product(form, left, right):
    return jnp.einsum(form, left, right, preferred_element_type=jnp.float32)


def low(values):
    return values.astype(jnp.bfloat16)


def wide(values):
    return values.astype(jnp.float32)


def body_planes(*arguments):
    tokens, cotangent, block_order = arguments[:3]
    weights_local = arguments[3:11]
    firsts = arguments[11:19]
    seconds = arguments[19:27]
    (
        latent_weight,
        query_up,
        keyval_up,
        output_weight,
        gate_weight,
        up_weight,
        down_weight,
        norm_gains,
    ) = weights_local
    shard_count = lax.axis_size(FSDP)
    context_count = lax.axis_size(CTX)
    tensor_count = lax.axis_size(TP)
    shard_place = lax.axis_index(FSDP)
    context_place = lax.axis_index(CTX)
    tensor_place = lax.axis_index(TP)
    _, local_length, width = tokens.shape
    half = width // shard_count
    share = local_length // tensor_count
    full_length = local_length * context_count
    block_length = full_length // block_order.shape[1]
    local_heads = HEADS // tensor_count
    owner_count = shard_count * context_count
    token_total = full_length * shard_count
    score_scale = 1.0 / math.sqrt(NOPE + ROPE)
    others = range(1, context_count)
    row_piece = width // owner_count

    def swap_fsdp(values):
        return lax.ppermute(values, FSDP, [(0, 1), (1, 0)])

    def swap_near(values):
        return lax.ppermute(values, TP, [(i, i ^ 1) for i in range(tensor_count)])

    def swap_far(values):
        return lax.ppermute(values, TP, [(i, i ^ 2) for i in range(tensor_count)])

    def shift(values, step):
        pairs = [(i, (i + step) % context_count) for i in range(context_count)]
        return lax.ppermute(values, CTX, pairs)

    def exchange(values):
        return lax.all_to_all(values, CTX, split_axis=0, concat_axis=0, tiled=False)

    def own_first(values):
        turned = jnp.concatenate([values[..., half:], values[..., :half]], axis=-1)
        return jnp.where(shard_place == 0, values, turned)

    def collect(values):
        return [values] + [shift(values, step) for step in others]

    def give_back(blocks):
        total = wide(blocks[0])
        for step in others:
            total = total + wide(shift(low(blocks[step]), -step))
        return total

    def over_tensor(values):
        near = jnp.concatenate([values, swap_near(values)], axis=0)
        return jnp.concatenate([near, swap_far(near)], axis=0)

    def sum_tensor(values):
        parts = [values[i * share : (i + 1) * share] for i in range(4)]
        got = wide(swap_near(jnp.concatenate([low(parts[1]), low(parts[3])], axis=0)))
        mine = wide(parts[0]) + got[:share]
        theirs = wide(parts[2]) + got[share:]
        return mine + wide(swap_far(low(theirs)))

    def gather_rows(shard):
        wide_shard = jnp.broadcast_to(shard[None], (context_count,) + shard.shape)
        own = exchange(wide_shard).reshape((-1,) + shard.shape[1:])
        return (own, swap_fsdp(own))

    def in_order(own, other):
        return jnp.where(
            shard_place == 0,
            jnp.concatenate([own, other], axis=0),
            jnp.concatenate([other, own], axis=0),
        )

    own_rows = lax.dynamic_slice_in_dim(tokens[0], tensor_place * share, share, 0)
    own_rows = own_first(own_rows)
    pieces = own_rows.reshape(share, shard_count, context_count, row_piece)
    pieces = pieces.transpose(2, 0, 1, 3).reshape(
        context_count, share, shard_count * row_piece
    )

    def piece_at(step):
        return lax.dynamic_index_in_dim(
            pieces, (context_place + step) % context_count, 0, False
        )

    feature_rows = jnp.concatenate(
        [piece_at(0)] + [shift(piece_at(step), step) for step in others], axis=0
    )
    latent_pair = jnp.concatenate([latent_weight, swap_fsdp(latent_weight)], axis=0)
    gain_wide = jnp.broadcast_to(norm_gains[None], (owner_count,) + norm_gains.shape)
    gain_full = wide(
        lax.all_to_all(gain_wide, (FSDP, CTX), split_axis=0, concat_axis=0).reshape(-1)
    )
    attend_gain = own_first(gain_full[:width])
    query_gain = gain_full[width : width + QR]
    keyval_gain = gain_full[width + QR : width + QR + KVR]
    feed_gain = own_first(gain_full[width + QR + KVR :])
    query_full = in_order(*gather_rows(query_up))
    keyval_full = in_order(*gather_rows(keyval_up))
    output_full = jnp.concatenate(gather_rows(output_weight), axis=0)

    inputs = wide(own_rows)
    input_inverse = lax.rsqrt(jnp.mean(inputs * inputs, axis=-1, keepdims=True) + norm_eps)
    gain_piece = lax.dynamic_index_in_dim(
        attend_gain.reshape(shard_count, context_count, row_piece), context_place, 1, False
    ).reshape(-1)
    scaled_rows = low(wide(feature_rows) * gain_piece)
    latent_part = product("kt,ta->ka", scaled_rows, latent_pair).reshape(
        context_count, share, -1
    )
    latent = give_back([latent_part[i] for i in range(context_count)]) * input_inverse

    def chunk_places(context_list, tensor_list):
        starts = jnp.stack(
            [
                ((context_place - c) % context_count) * local_length
                + (tensor_place ^ t) * share
                for t in tensor_list
                for c in context_list
            ]
        )
        bases = jnp.take(block_order[0], starts // block_length) * block_length
        bases = bases + starts % block_length
        return (bases[:, None] + jnp.arange(share, dtype=jnp.int32)[None, :]).reshape(-1)

    key_places = chunk_places(range(context_count), range(tensor_count))
    query_places = chunk_places((0,), range(tensor_count))
    cosine_table, sine_table = rope_tables(wide(query_places))
    cosine_own, sine_own = cosine_table[:share], sine_table[:share]

    query_latent = low(norm_apply(latent[:, :QR], query_gain))
    keyval_latent = low(norm_apply(latent[:, QR : QR + KVR], keyval_gain))
    key_rope = low(rotate(latent[:, QR + KVR :], cosine_own, sine_own))
    key_rows = over_tensor(
        jnp.concatenate(collect(jnp.concatenate([keyval_latent, key_rope], axis=1)), axis=0)
    )
    query_rows = over_tensor(query_latent)
    keyval_rows = key_rows[:, :KVR]
    rope_rows = key_rows[:, KVR:]

    query_pre = product("lr,re->le", query_rows, query_full).reshape(
        local_length, local_heads, NOPE + ROPE
    )
    queries = low(
        jnp.concatenate(
            [
                query_pre[..., :NOPE],
                rotate(query_pre[..., NOPE:], cosine_table[:, None, :], sine_table[:, None, :]),
            ],
            axis=-1,
        )
    )
    keyval = low(product("lr,re->le", keyval_rows, keyval_full)).reshape(
        full_length, local_heads, NOPE + VDIM
    )
    key_nope = keyval[..., :NOPE]
    value_rows = keyval[..., NOPE:]
    visible = key_places[None, None, :] <= query_places[None, :, None]

    def score_table():
        raw_scores = product("ihd,jhd->hij", queries[..., :NOPE], key_nope)
        raw_scores = raw_scores + product("ihd,jd->hij", queries[..., NOPE:], rope_rows)
        return jnp.where(visible, raw_scores * score_scale, -1e30)

    scores = score_table()
    row_max = jnp.max(scores, axis=-1, keepdims=True)
    exponent = jnp.exp(scores - row_max)
    row_sum = jnp.sum(exponent, axis=-1, keepdims=True)
    probs_low = low(exponent / row_sum)
    attended = low(product("hij,jhd->ihd", probs_low, value_rows)).reshape(
        local_length, local_heads * VDIM
    )
    branch = sum_tensor(product("yz,hz->yh", attended, output_full))
    hidden = inputs + residual_scale * branch
    normed_feed = low(norm_apply(hidden, feed_gain))

    def spread(values):
        near = collect(values)
        far = [swap_far(item) for item in near]
        return jnp.concatenate(near + far, axis=0)

    def fold(values):
        count = share * context_count
        far = [
            wide(swap_far(low(values[count + i * share : count + (i + 1) * share])))
            for i in range(context_count)
        ]
        return give_back(
            [wide(values[i * share : (i + 1) * share]) + far[i] for i in range(context_count)]
        )

    unit_count = gate_weight.shape[1]
    unit_step = unit_count // context_count // 128 * 128
    unit_width = unit_count - unit_step * (context_count - 1)

    def fetch_units(shard):
        windows = jnp.stack(
            [shard[:, i * unit_step : i * unit_step + unit_width] for i in range(context_count)]
        )
        own = exchange(windows).reshape(-1, unit_width)
        own = jnp.concatenate([own, swap_fsdp(own)], axis=0)
        return (own, swap_near(own))

    unit_limit = jnp.where(context_place == context_count - 1, unit_width, unit_step)
    unit_mask = jnp.arange(unit_width)[None, :] < unit_limit
    gate_pair = fetch_units(gate_weight)
    up_pair = fetch_units(up_weight)
    down_pair = fetch_units(down_weight)

    incoming = own_first(
        wide(lax.dynamic_slice_in_dim(cotangent[0], tensor_place * share, share, 0))
    )
    seed_rows = spread(low(residual_scale * incoming))
    feed_rows = spread(normed_feed)

    out_part = 0.0
    back_part = 0.0
    weight_parts = []
    for gate_own, up_own, down_own in zip(gate_pair, up_pair, down_pair):
        gate = product("wt,tu->wu", feed_rows, gate_own)
        upward = product("wt,tu->wu", feed_rows, up_own)
        sigmoid_gate = jax.nn.sigmoid(gate)
        silu_gate = jnp.where(unit_mask, gate * sigmoid_gate, 0.0)
        activated = low(silu_gate * upward)
        act_grad = jnp.where(unit_mask, product("wt,tu->wu", seed_rows, down_own), 0.0)
        gate_grad = low(act_grad * upward * sigmoid_gate * (1.0 + gate * (1.0 - sigmoid_gate)))
        upward_grad = low(act_grad * silu_gate)
        out_part = out_part + product("mw,vw->mv", activated, down_own)
        back_part = back_part + product("mw,vw->mv", gate_grad, gate_own)
        back_part = back_part + product("mw,vw->mv", upward_grad, up_own)
        weight_parts.append(
            (
                product("bn,bt->nt", feed_rows, gate_grad),
                product("bn,bt->nt", feed_rows, upward_grad),
                product("bn,bt->nt", seed_rows, activated),
            )
        )

    normed_back = fold(back_part)
    feed_total = fold(out_part)
    output_rows = own_first(hidden + residual_scale * feed_total)

    def sum_units(own, other):
        total = own + wide(swap_near(low(other)))
        total = total[:half] + wide(swap_fsdp(low(total[half:])))
        got = wide(exchange(low(total).reshape(context_count, row_piece, unit_width)))
        return jnp.concatenate(
            [got[i][:, :unit_step] for i in range(context_count - 1)] + [got[-1]], axis=1
        )

    def sum_rows(own, other):
        total = own + wide(swap_fsdp(low(other)))
        got = exchange(low(total).reshape((context_count, -1) + own.shape[1:]))
        return jnp.sum(wide(got), axis=0)

    hidden_back, feed_gain_rows = norm_back(hidden, feed_gain, normed_back)
    hidden_grad = incoming + hidden_back
    branch_grad = over_tensor(low(residual_scale * hidden_grad))
    attended_grad = low(product("nq,qk->nk", branch_grad, output_full)).reshape(
        local_length, local_heads, VDIM
    )
    output_part = product("xg,xn->gn", branch_grad, attended)

    scores = score_table()
    attend_probs = jnp.exp(scores - row_max) / row_sum
    probs_low = low(attend_probs)
    prob_grad = product("ihd,jhd->hij", attended_grad, value_rows)
    score_grad = low(
        attend_probs * (prob_grad - jnp.sum(attend_probs * prob_grad, axis=-1, keepdims=True))
    )
    query_grad = (
        jnp.concatenate(
            [
                product("hij,jhd->ihd", score_grad, key_nope),
                product("hij,jd->ihd", score_grad, rope_rows),
            ],
            axis=-1,
        )
        * score_scale
    )
    key_nope_grad = product("hij,ihd->jhd", score_grad, queries[..., :NOPE]) * score_scale
    value_grad = product("hij,ihd->jhd", probs_low, attended_grad)
    rope_grad = product("hij,ihd->jd", score_grad, queries[..., NOPE:]) * score_scale
    keyval_grad = low(jnp.concatenate([key_nope_grad, value_grad], axis=-1)).reshape(
        full_length, local_heads * (NOPE + VDIM)
    )
    key_back = jnp.concatenate(
        [product("le,re->lr", keyval_grad, keyval_full), rope_grad], axis=1
    )
    count = full_length // 2
    key_back = key_back[:count] + wide(swap_far(low(key_back[count:])))
    count = count // 2
    key_back = key_back[:count] + wide(swap_near(low(key_back[count:])))
    key_back = give_back([key_back[i * share : (i + 1) * share] for i in range(context_count)])

    query_pre_grad = low(
        jnp.concatenate(
            [
                query_grad[..., :NOPE],
                rotate_back(
                    query_grad[..., NOPE:], cosine_table[:, None, :], sine_table[:, None, :]
                ),
            ],
            axis=-1,
        ).reshape(local_length, local_heads * (NOPE + ROPE))
    )
    query_back = sum_tensor(product("le,re->lr", query_pre_grad, query_full))
    query_part = product("lr,le->re", query_rows, query_pre_grad)
    keyval_part = product("lr,le->re", keyval_rows, keyval_grad)

    query_lat_grad, query_gain_rows = norm_back(latent[:, :QR], query_gain, query_back)
    keyval_lat_grad, keyval_gain_rows = norm_back(
        latent[:, QR : QR + KVR], keyval_gain, key_back[:, :KVR]
    )
    rope_lat_grad = rotate_back(key_back[:, KVR:], cosine_own, sine_own)
    latent_grad = jnp.concatenate([query_lat_grad, keyval_lat_grad, rope_lat_grad], axis=-1)
    latent_grad_rows = jnp.concatenate(collect(low(latent_grad * input_inverse)), axis=0)
    latent_sum_part = product("po,pm->om", scaled_rows, latent_grad_rows)
    normed_grad_part = low(product("cj,kj->ck", latent_grad_rows, latent_pair)).reshape(
        context_count, share, shard_count * row_piece
    )
    returned = jnp.stack(
        [normed_grad_part[0]] + [shift(normed_grad_part[step], -step) for step in others]
    )
    normed_grad = jnp.stack(
        [
            lax.dynamic_index_in_dim(returned, (i - context_place) % context_count, 0, False)
            for i in range(context_count)
        ]
    )
    normed_grad = (
        wide(normed_grad)
        .reshape(context_count, share, shard_count, row_piece)
        .transpose(1, 2, 0, 3)
        .reshape(share, width)
        / input_inverse
    )
    input_back, attend_gain_rows = norm_back(inputs, attend_gain, normed_grad)
    input_grad = own_first(hidden_grad + input_back)

    gain_sum = jnp.concatenate(
        [
            own_first(jnp.sum(attend_gain_rows, axis=0)),
            jnp.sum(query_gain_rows, axis=0),
            jnp.sum(keyval_gain_rows, axis=0),
            own_first(jnp.sum(feed_gain_rows, axis=0)),
        ]
    )
    gain_sum = gain_sum.reshape(owner_count, -1)
    gain_sum = gain_sum + swap_near(gain_sum)
    gain_sum = gain_sum + swap_far(gain_sum)
    gain_sum = jnp.sum(
        lax.all_to_all(gain_sum, (FSDP, CTX), split_axis=0, concat_axis=0), axis=0
    )

    latent_sum = low(
        latent_sum_part[:row_piece] + wide(swap_fsdp(low(latent_sum_part[row_piece:])))
    )
    latent_sum = low(wide(latent_sum) + wide(swap_near(latent_sum)))
    latent_sum = wide(latent_sum) + wide(swap_far(latent_sum))

    def halves(values):
        stacked = values.reshape((shard_count, -1) + values.shape[1:])
        return (
            lax.dynamic_index_in_dim(stacked, shard_place, 0, False),
            lax.dynamic_index_in_dim(stacked, 1 - shard_place, 0, False),
        )

    summed = (
        latent_sum,
        sum_rows(*halves(query_part)),
        sum_rows(*halves(keyval_part)),
        sum_rows(output_part[:half], output_part[half:]),
        sum_units(weight_parts[0][0], weight_parts[1][0]),
        sum_units(weight_parts[0][1], weight_parts[1][1]),
        sum_units(weight_parts[0][2], weight_parts[1][2]),
        gain_sum,
    )
    shards = tuple(item / token_total for item in summed)
    lead_flag = wide(tensor_place == 0)
    local_square = lead_flag * (jnp.sum(shards[0] * shards[0]) + jnp.sum(shards[7] * shards[7]))
    for shard_grad in shards[1:7]:
        local_square = local_square + jnp.sum(shard_grad * shard_grad)
    square = jnp.full((8, 128), local_square)
    square = square + swap_near(square)
    square = square + swap_far(square)
    square = square + swap_fsdp(square)
    around = [shift(square, step) for step in others]
    square = (square + around[1]) + (around[0] + around[2])
    grad_norm = jnp.sqrt(square[0, 0])
    factor = clip_level / jnp.maximum(grad_norm, clip_level)
    stepped = [
        adam_step(
            weights_local[i], shards[i], firsts[i], seconds[i], factor, i < 7
        )
        for i in range(8)
    ]
    return (
        (output_rows[None], input_grad[None])
        + shards
        + (grad_norm,)
        + tuple(item[0] for item in stepped)
        + tuple(item[1] for item in stepped)
        + tuple(item[2] for item in stepped)
    )


def solution(mesh):
    sizes = dict(mesh.shape)
    planes = sizes[FSDP] == 2 and sizes[CTX] == 4 and sizes[TP] == 4
    body = body_planes if planes else body_gathered
    placed = (
        P(FSDP, CTX, None),
        P(FSDP, CTX, None),
        P(FSDP, None),
        ROWS,
        SPLIT,
        SPLIT,
        SPLIT,
        SPLIT,
        SPLIT,
        SPLIT,
        GAIN,
        ROWS,
        SPLIT,
        SPLIT,
        SPLIT,
        SPLIT,
        SPLIT,
        SPLIT,
        GAIN,
        ROWS,
        SPLIT,
        SPLIT,
        SPLIT,
        SPLIT,
        SPLIT,
        SPLIT,
        GAIN,
    )
    return jax.shard_map(
        body,
        mesh=mesh,
        in_specs=placed,
        out_specs=(
            P(FSDP, (CTX, TP), None),
            P(FSDP, (CTX, TP), None),
            ROWS,
            SPLIT,
            SPLIT,
            SPLIT,
            SPLIT,
            SPLIT,
            SPLIT,
            GAIN,
            P(),
            ROWS,
            SPLIT,
            SPLIT,
            SPLIT,
            SPLIT,
            SPLIT,
            SPLIT,
            GAIN,
            ROWS,
            SPLIT,
            SPLIT,
            SPLIT,
            SPLIT,
            SPLIT,
            SPLIT,
            GAIN,
            ROWS,
            SPLIT,
            SPLIT,
            SPLIT,
            SPLIT,
            SPLIT,
            SPLIT,
            GAIN,
        ),
        check_vma=False,
    )
```

```python
import math

import jax
import jax.numpy as jnp
from jax import lax
from jax.sharding import PartitionSpec as P

HEADS = 40
NOPE = 64
ROPE = 32
VDIM = 64
QR = 768
KVR = 256

FSDP = "fsdp"
CTX = "ctx"
TP = "tp"
SPLIT = P((FSDP, CTX), TP)
ROWS = P((FSDP, CTX), None)
GAIN = P((FSDP, CTX))


residual_scale = 1.4 / math.sqrt(62.0)
norm_eps = 1e-05
clip_level = 0.01
beta_first = 0.5
beta_second = 0.5
learn_rate = 0.05
decay_rate = 0.1
adam_eps = 1e-08
step_count = 3.0


def contraction_product(form, left, right):
    return jnp.einsum(form, left, right, preferred_element_type=jnp.float32)


def norm_apply(values, norm_gain):
    inverse = lax.rsqrt(jnp.mean(values * values, axis=-1, keepdims=True) + norm_eps)
    return values * inverse * norm_gain


def norm_back(values, norm_gain, incoming):
    inverse = lax.rsqrt(jnp.mean(values * values, axis=-1, keepdims=True) + norm_eps)
    unit_rows = values * inverse
    scaled = incoming * norm_gain
    value_grad = inverse * (
        scaled - unit_rows * jnp.mean(unit_rows * scaled, axis=-1, keepdims=True)
    )
    return (value_grad, incoming * unit_rows)


def rope_tables(positions):
    half_size = ROPE // 2
    frequency = jnp.exp(
        -math.log(10000.0) * (2.0 * jnp.arange(half_size, dtype=jnp.float32) / ROPE)
    )
    angles = positions[..., None] * frequency
    return (jnp.cos(angles), jnp.sin(angles))


def rotate(values, cosine_table, sine_table):
    half_size = values.shape[-1] // 2
    front_half = values[..., :half_size]
    back_half = values[..., half_size:]
    return jnp.concatenate(
        [
            front_half * cosine_table - back_half * sine_table,
            back_half * cosine_table + front_half * sine_table,
        ],
        axis=-1,
    )


def rotate_back(values, cosine_table, sine_table):
    half_size = values.shape[-1] // 2
    front_half = values[..., :half_size]
    back_half = values[..., half_size:]
    return jnp.concatenate(
        [
            front_half * cosine_table + back_half * sine_table,
            back_half * cosine_table - front_half * sine_table,
        ],
        axis=-1,
    )


def adam_step(weight, gradient, first_old, second_old, factor, decayed):
    clipped = gradient * factor
    first_new = beta_first * first_old + (1.0 - beta_first) * clipped
    second_new = beta_second * second_old + (1.0 - beta_second) * clipped * clipped
    first_hat = first_new / (1.0 - beta_first**step_count)
    second_hat = second_new / (1.0 - beta_second**step_count)
    change = first_hat / (jnp.sqrt(second_hat) + adam_eps)
    if decayed:
        change = change + decay_rate * weight.astype(jnp.float32)
    return (first_new, second_new, -learn_rate * change)


def body_gathered(
    tokens,
    cotangent,
    block_order,
    latent_weight,
    query_up,
    keyval_up,
    output_weight,
    gate_weight,
    up_weight,
    down_weight,
    norm_gains,
    first_latent,
    first_query,
    first_keyval,
    first_output,
    first_gate,
    first_up,
    first_down,
    first_gains,
    second_latent,
    second_query,
    second_keyval,
    second_output,
    second_gate,
    second_up,
    second_down,
    second_gains,
):
    context_count = lax.axis_size(CTX)
    tensor_count = lax.axis_size(TP)
    shard_count = lax.axis_size(FSDP)
    context_place = lax.axis_index(CTX)
    tensor_place = lax.axis_index(TP)
    sequences, local_length, width = tokens.shape
    full_length = local_length * context_count
    share_length = local_length // tensor_count
    share_start = tensor_place * share_length
    local_heads = HEADS // tensor_count
    block_length = full_length // (2 * context_count)
    token_total = sequences * full_length * shard_count
    owner_count = shard_count * context_count
    row_piece = width // (owner_count * tensor_count)
    score_scale = 1.0 / math.sqrt(NOPE + ROPE)
    gathered = (
        lax.all_gather(latent_weight, (FSDP, CTX), axis=0, tiled=True),
        lax.all_gather(query_up, (FSDP, CTX), axis=0, tiled=True),
        lax.all_gather(keyval_up, (FSDP, CTX), axis=0, tiled=True),
        lax.all_gather(output_weight, (FSDP, CTX), axis=0, tiled=True),
        lax.all_gather(gate_weight, (FSDP, CTX), axis=0, tiled=True),
        lax.all_gather(up_weight, (FSDP, CTX), axis=0, tiled=True),
        lax.all_gather(down_weight, (FSDP, CTX), axis=0, tiled=True),
        lax.all_gather(norm_gains, (FSDP, CTX), axis=0, tiled=True),
    )
    (
        latent_weight_complete,
        query_full,
        keyval_full,
        output_weight_complete,
        gate_weight_complete,
        up_weight_complete,
        down_weight_complete,
        gain_full,
    ) = gathered
    gain_float = gain_full.astype(jnp.float32)
    attend_gain = gain_float[:width]
    query_gain = gain_float[width : width + QR]
    keyval_gain = gain_float[width + QR : width + QR + KVR]
    feed_gain = gain_float[width + QR + KVR :]
    offsets = jnp.arange(block_length, dtype=jnp.int32)
    position_all = (block_order[:, :, None] * block_length + offsets[None, None, :]).reshape(
        sequences, full_length
    )
    position_all = position_all.astype(jnp.float32)
    position_here = lax.dynamic_slice_in_dim(
        position_all, context_place * local_length, local_length, 1
    )
    cosine_here, sine_here = rope_tables(position_here)
    inputs = tokens.astype(jnp.float32)
    normalized_input = norm_apply(inputs, attend_gain).astype(jnp.bfloat16)
    latent_projection = contraction_product("kai,it->kat", normalized_input, latent_weight_complete)
    query_latent = norm_apply(latent_projection[..., :QR], query_gain).astype(jnp.bfloat16)
    keyval_latent = norm_apply(latent_projection[..., QR : QR + KVR], keyval_gain).astype(
        jnp.bfloat16
    )
    key_rope = rotate(latent_projection[..., QR + KVR :], cosine_here, sine_here).astype(
        jnp.bfloat16
    )
    query_pre = contraction_product("slr,re->sle", query_latent, query_full).reshape(
        sequences, local_length, local_heads, NOPE + ROPE
    )
    queries = jnp.concatenate(
        [
            query_pre[..., :NOPE],
            rotate(query_pre[..., NOPE:], cosine_here[:, :, None, :], sine_here[:, :, None, :]),
        ],
        axis=-1,
    ).astype(jnp.bfloat16)
    keyval = contraction_product("slr,re->sle", keyval_latent, keyval_full).astype(jnp.bfloat16)
    keyval_all, rope_all = (
        lax.all_gather(keyval, CTX, axis=1, tiled=True),
        lax.all_gather(key_rope, CTX, axis=1, tiled=True),
    )
    keyval_heads = keyval_all.reshape(sequences, full_length, local_heads, NOPE + VDIM)
    key_nope = keyval_heads[..., :NOPE]
    value_rows = keyval_heads[..., NOPE:]
    visible = position_all[:, None, None, :] <= position_here[:, None, :, None]

    def score_table():
        raw_scores = contraction_product("sihd,sjhd->shij", queries[..., :NOPE], key_nope)
        raw_scores = raw_scores + contraction_product(
            "sihd,sjd->shij", queries[..., NOPE:], rope_all
        )
        return jnp.where(visible, raw_scores * score_scale, -1e30)

    scores = score_table()
    row_max = jnp.max(scores, axis=-1, keepdims=True)
    exponent = jnp.exp(scores - row_max)
    row_sum = jnp.sum(exponent, axis=-1, keepdims=True)
    probs_low = (exponent / row_sum).astype(jnp.bfloat16)
    attention_result = contraction_product("shij,sjhd->sihd", probs_low, value_rows)
    attention_result = attention_result.reshape(sequences, local_length, local_heads * VDIM).astype(
        jnp.bfloat16
    )
    branch_portion = contraction_product("nyz,hz->nyh", attention_result, output_weight_complete)
    branch = lax.psum(branch_portion, TP)
    hidden = inputs + residual_scale * branch
    normalized_feed_input = norm_apply(hidden, feed_gain).astype(jnp.bfloat16)
    gate_activation = contraction_product(
        "ewt,tu->ewu", normalized_feed_input, gate_weight_complete
    )
    upward_projection = contraction_product(
        "ewt,tu->ewu", normalized_feed_input, up_weight_complete
    )
    sigmoid_gate = jax.nn.sigmoid(gate_activation)
    silu_gate = gate_activation * sigmoid_gate
    activation_rows = (silu_gate * upward_projection).astype(jnp.bfloat16)
    feed_portion = contraction_product("umw,vw->umv", activation_rows, down_weight_complete)
    feed_total = lax.psum(feed_portion.astype(jnp.bfloat16), TP).astype(jnp.float32)
    output_rows = lax.dynamic_slice_in_dim(
        hidden + residual_scale * feed_total, share_start, share_length, 1
    )
    incoming = cotangent.astype(jnp.float32)
    feed_gradient_start = (residual_scale * incoming).astype(jnp.bfloat16)
    activation_gradient = contraction_product(
        "ewt,tu->ewu", feed_gradient_start, down_weight_complete
    )
    gate_gradient_rows = (
        activation_gradient
        * upward_projection
        * sigmoid_gate
        * (1.0 + gate_activation * (1.0 - sigmoid_gate))
    ).astype(jnp.bfloat16)
    upward_gradient_rows = (activation_gradient * silu_gate).astype(jnp.bfloat16)
    down_weight_gradient = contraction_product("ubn,ubt->nt", feed_gradient_start, activation_rows)
    gate_weight_gradient = contraction_product(
        "ubn,ubt->nt", normalized_feed_input, gate_gradient_rows
    )
    upward_weight_gradient = contraction_product(
        "ubn,ubt->nt", normalized_feed_input, upward_gradient_rows
    )
    normalized_gradient_portion = contraction_product(
        "umw,vw->umv", gate_gradient_rows, gate_weight_complete
    ) + contraction_product("umw,vw->umv", upward_gradient_rows, up_weight_complete)
    normed_grad = lax.psum(normalized_gradient_portion, TP)
    hidden_back, gain_rows = norm_back(hidden, feed_gain, normed_grad)
    hidden_grad = incoming + hidden_back
    feed_gain_part = jnp.sum(
        lax.dynamic_slice_in_dim(gain_rows, share_start, share_length, 1), axis=(0, 1)
    )
    branch_gradient_part = (residual_scale * hidden_grad).astype(jnp.bfloat16)
    hidden_grad_share = lax.dynamic_slice_in_dim(hidden_grad, share_start, share_length, 1)
    output_weight_gradient = contraction_product(
        "zxg,zxn->gn", branch_gradient_part, attention_result
    )
    attention_result_gradient = contraction_product(
        "rnq,qk->rnk", branch_gradient_part, output_weight_complete
    ).astype(jnp.bfloat16)
    attention_result_gradient = attention_result_gradient.reshape(
        sequences, local_length, local_heads, VDIM
    )
    scores = score_table()
    attend_probs = jnp.exp(scores - row_max) / row_sum
    probs_low = attend_probs.astype(jnp.bfloat16)
    prob_grad = contraction_product("sihd,sjhd->shij", attention_result_gradient, value_rows)
    score_grad = (
        attend_probs * (prob_grad - jnp.sum(attend_probs * prob_grad, axis=-1, keepdims=True))
    ).astype(jnp.bfloat16)
    query_grad = (
        jnp.concatenate(
            [
                contraction_product("shij,sjhd->sihd", score_grad, key_nope),
                contraction_product("shij,sjd->sihd", score_grad, rope_all),
            ],
            axis=-1,
        )
        * score_scale
    )
    key_nope_grad = (
        contraction_product("shij,sihd->sjhd", score_grad, queries[..., :NOPE]) * score_scale
    )
    value_grad = contraction_product("shij,sihd->sjhd", probs_low, attention_result_gradient)
    rope_grad_all = (
        contraction_product("shij,sihd->sjd", score_grad, queries[..., NOPE:]) * score_scale
    )
    keyval_grad_all = jnp.concatenate([key_nope_grad, value_grad], axis=-1)
    keyval_grad_all = keyval_grad_all.reshape(sequences, full_length, local_heads * (NOPE + VDIM))
    keyval_grad, rope_grad = (
        lax.psum_scatter(
            keyval_grad_all.astype(jnp.bfloat16), CTX, scatter_dimension=1, tiled=True
        ).astype(jnp.float32),
        lax.psum_scatter(
            rope_grad_all.astype(jnp.bfloat16), CTX, scatter_dimension=1, tiled=True
        ).astype(jnp.float32),
    )
    query_pre_grad = jnp.concatenate(
        [
            query_grad[..., :NOPE],
            rotate_back(
                query_grad[..., NOPE:], cosine_here[:, :, None, :], sine_here[:, :, None, :]
            ),
        ],
        axis=-1,
    )
    query_pre_grad = query_pre_grad.reshape(
        sequences, local_length, local_heads * (NOPE + ROPE)
    ).astype(jnp.bfloat16)
    grad_query = contraction_product("slr,sle->re", query_latent, query_pre_grad)
    keyval_grad_low = keyval_grad.astype(jnp.bfloat16)
    grad_keyval = contraction_product("slr,sle->re", keyval_latent, keyval_grad_low)
    latent_grad_part = jnp.concatenate(
        [
            contraction_product("sle,re->slr", query_pre_grad, query_full),
            contraction_product("sle,re->slr", keyval_grad_low, keyval_full),
            rope_grad,
        ],
        axis=-1,
    )
    latent_grad_sum, feed_gain_grad = (
        lax.psum(latent_grad_part.astype(jnp.bfloat16), TP).astype(jnp.float32),
        lax.psum(feed_gain_part.astype(jnp.bfloat16), TP).astype(jnp.float32),
    )
    query_lat_grad, query_gain_rows = norm_back(
        latent_projection[..., :QR], query_gain, latent_grad_sum[..., :QR]
    )
    keyval_lat_grad, keyval_gain_rows = norm_back(
        latent_projection[..., QR : QR + KVR], keyval_gain, latent_grad_sum[..., QR : QR + KVR]
    )
    rope_lat_grad = rotate_back(latent_grad_sum[..., QR + KVR :], cosine_here, sine_here)
    latent_gradient_rows = jnp.concatenate(
        [query_lat_grad, keyval_lat_grad, rope_lat_grad], axis=-1
    ).astype(jnp.bfloat16)
    normed_split = normalized_input.reshape(
        sequences, local_length, owner_count, tensor_count, row_piece
    )
    normed_pick = lax.dynamic_index_in_dim(normed_split, tensor_place, 3, False)
    normed_pick = normed_pick.reshape(sequences, local_length, owner_count * row_piece)
    latent_weight_gradient = contraction_product("pjo,pjm->om", normed_pick, latent_gradient_rows)
    normalized_attention_gradient = contraction_product(
        "ycj,kj->yck", latent_gradient_rows, latent_weight_complete
    )
    input_back, attend_gain_rows = norm_back(inputs, attend_gain, normalized_attention_gradient)
    input_grad = hidden_grad_share + lax.dynamic_slice_in_dim(
        input_back, share_start, share_length, 1
    )
    gain_grad_full = jnp.concatenate(
        [
            jnp.sum(attend_gain_rows, axis=(0, 1)),
            jnp.sum(query_gain_rows, axis=(0, 1)),
            jnp.sum(keyval_gain_rows, axis=(0, 1)),
            feed_gain_grad,
        ],
        axis=0,
    )
    summed = (
        lax.psum_scatter(
            latent_weight_gradient.astype(jnp.bfloat16),
            (FSDP, CTX),
            scatter_dimension=0,
            tiled=True,
        ).astype(jnp.float32),
        lax.psum_scatter(
            grad_query.astype(jnp.bfloat16), (FSDP, CTX), scatter_dimension=0, tiled=True
        ).astype(jnp.float32),
        lax.psum_scatter(
            grad_keyval.astype(jnp.bfloat16), (FSDP, CTX), scatter_dimension=0, tiled=True
        ).astype(jnp.float32),
        lax.psum_scatter(
            output_weight_gradient.astype(jnp.bfloat16),
            (FSDP, CTX),
            scatter_dimension=0,
            tiled=True,
        ).astype(jnp.float32),
        lax.psum_scatter(
            gate_weight_gradient.astype(jnp.bfloat16),
            (FSDP, CTX),
            scatter_dimension=0,
            tiled=True,
        ).astype(jnp.float32),
        lax.psum_scatter(
            upward_weight_gradient.astype(jnp.bfloat16),
            (FSDP, CTX),
            scatter_dimension=0,
            tiled=True,
        ).astype(jnp.float32),
        lax.psum_scatter(
            down_weight_gradient.astype(jnp.bfloat16),
            (FSDP, CTX),
            scatter_dimension=0,
            tiled=True,
        ).astype(jnp.float32),
        lax.psum_scatter(
            gain_grad_full.astype(jnp.bfloat16), (FSDP, CTX), scatter_dimension=0, tiled=True
        ).astype(jnp.float32),
    )
    latent_owned = lax.all_gather(summed[0].astype(jnp.bfloat16), TP, axis=0, tiled=True).astype(
        jnp.float32
    )
    shards = tuple((shard_grad / token_total for shard_grad in (latent_owned,) + tuple(summed[1:])))
    lead_flag = (tensor_place == 0).astype(jnp.float32)
    local_square = lead_flag * (jnp.sum(shards[0] * shards[0]) + jnp.sum(shards[7] * shards[7]))
    for shard_grad in shards[1:7]:
        local_square = local_square + jnp.sum(shard_grad * shard_grad)
    total_square = lax.psum(local_square, (FSDP, CTX, TP))
    grad_norm = jnp.sqrt(total_square)
    factor = clip_level / jnp.maximum(grad_norm, clip_level)
    weights_local = (
        latent_weight,
        query_up,
        keyval_up,
        output_weight,
        gate_weight,
        up_weight,
        down_weight,
        norm_gains,
    )
    firsts = (
        first_latent,
        first_query,
        first_keyval,
        first_output,
        first_gate,
        first_up,
        first_down,
        first_gains,
    )
    seconds = (
        second_latent,
        second_query,
        second_keyval,
        second_output,
        second_gate,
        second_up,
        second_down,
        second_gains,
    )
    new_first = []
    new_second = []
    changes = []
    for index_item in range(8):
        first_new, second_new, change = adam_step(
            weights_local[index_item],
            shards[index_item],
            firsts[index_item],
            seconds[index_item],
            factor,
            index_item < 7,
        )
        new_first.append(first_new)
        new_second.append(second_new)
        changes.append(change)
    return (
        (output_rows, input_grad)
        + shards
        + (grad_norm,)
        + tuple(new_first)
        + tuple(new_second)
        + tuple(changes)
    )


def product(form, left, right):
    return jnp.einsum(form, left, right, preferred_element_type=jnp.float32)


def low(values):
    return values.astype(jnp.bfloat16)


def wide(values):
    return values.astype(jnp.float32)


def body_planes(*arguments):
    tokens, cotangent, block_order = arguments[:3]
    weights_local = arguments[3:11]
    firsts = arguments[11:19]
    seconds = arguments[19:27]
    (
        latent_weight,
        query_up,
        keyval_up,
        output_weight,
        gate_weight,
        up_weight,
        down_weight,
        norm_gains,
    ) = weights_local
    shard_count = lax.axis_size(FSDP)
    context_count = lax.axis_size(CTX)
    tensor_count = lax.axis_size(TP)
    shard_place = lax.axis_index(FSDP)
    context_place = lax.axis_index(CTX)
    tensor_place = lax.axis_index(TP)
    _, local_length, width = tokens.shape
    half = width // shard_count
    share = local_length // tensor_count
    full_length = local_length * context_count
    block_length = full_length // block_order.shape[1]
    local_heads = HEADS // tensor_count
    owner_count = shard_count * context_count
    token_total = full_length * shard_count
    score_scale = 1.0 / math.sqrt(NOPE + ROPE)
    others = range(1, context_count)
    row_piece = width // owner_count

    def swap_fsdp(values):
        return lax.ppermute(values, FSDP, [(0, 1), (1, 0)])

    def swap_near(values):
        return lax.ppermute(values, TP, [(i, i ^ 1) for i in range(tensor_count)])

    def swap_far(values):
        return lax.ppermute(values, TP, [(i, i ^ 2) for i in range(tensor_count)])

    def shift(values, step):
        pairs = [(i, (i + step) % context_count) for i in range(context_count)]
        return lax.ppermute(values, CTX, pairs)

    def exchange(values):
        return lax.all_to_all(values, CTX, split_axis=0, concat_axis=0, tiled=False)

    def own_first(values):
        turned = jnp.concatenate([values[..., half:], values[..., :half]], axis=-1)
        return jnp.where(shard_place == 0, values, turned)

    def collect(values):
        return [values] + [shift(values, step) for step in others]

    def give_back(blocks):
        total = wide(blocks[0])
        for step in others:
            total = total + wide(shift(low(blocks[step]), -step))
        return total

    def over_tensor(values):
        near = jnp.concatenate([values, swap_near(values)], axis=0)
        return jnp.concatenate([near, swap_far(near)], axis=0)

    def sum_tensor(values):
        parts = [values[i * share : (i + 1) * share] for i in range(4)]
        got = wide(swap_near(jnp.concatenate([low(parts[1]), low(parts[3])], axis=0)))
        mine = wide(parts[0]) + got[:share]
        theirs = wide(parts[2]) + got[share:]
        return mine + wide(swap_far(low(theirs)))

    def gather_rows(shard):
        wide_shard = jnp.broadcast_to(shard[None], (context_count,) + shard.shape)
        own = exchange(wide_shard).reshape((-1,) + shard.shape[1:])
        return (own, swap_fsdp(own))

    def in_order(own, other):
        return jnp.where(
            shard_place == 0,
            jnp.concatenate([own, other], axis=0),
            jnp.concatenate([other, own], axis=0),
        )

    own_rows = lax.dynamic_slice_in_dim(tokens[0], tensor_place * share, share, 0)
    own_rows = own_first(own_rows)
    pieces = own_rows.reshape(share, shard_count, context_count, row_piece)
    pieces = pieces.transpose(2, 0, 1, 3).reshape(
        context_count, share, shard_count * row_piece
    )

    def piece_at(step):
        return lax.dynamic_index_in_dim(
            pieces, (context_place + step) % context_count, 0, False
        )

    feature_rows = jnp.concatenate(
        [piece_at(0)] + [shift(piece_at(step), step) for step in others], axis=0
    )
    latent_pair = jnp.concatenate([latent_weight, swap_fsdp(latent_weight)], axis=0)
    gain_wide = jnp.broadcast_to(norm_gains[None], (owner_count,) + norm_gains.shape)
    gain_full = wide(
        lax.all_to_all(gain_wide, (FSDP, CTX), split_axis=0, concat_axis=0).reshape(-1)
    )
    attend_gain = own_first(gain_full[:width])
    query_gain = gain_full[width : width + QR]
    keyval_gain = gain_full[width + QR : width + QR + KVR]
    feed_gain = own_first(gain_full[width + QR + KVR :])
    query_full = in_order(*gather_rows(query_up))
    keyval_full = in_order(*gather_rows(keyval_up))
    output_full = jnp.concatenate(gather_rows(output_weight), axis=0)

    inputs = wide(own_rows)
    input_inverse = lax.rsqrt(jnp.mean(inputs * inputs, axis=-1, keepdims=True) + norm_eps)
    gain_piece = lax.dynamic_index_in_dim(
        attend_gain.reshape(shard_count, context_count, row_piece), context_place, 1, False
    ).reshape(-1)
    scaled_rows = low(wide(feature_rows) * gain_piece)
    latent_part = product("kt,ta->ka", scaled_rows, latent_pair).reshape(
        context_count, share, -1
    )
    latent = give_back([latent_part[i] for i in range(context_count)]) * input_inverse

    def chunk_places(context_list, tensor_list):
        starts = jnp.stack(
            [
                ((context_place - c) % context_count) * local_length
                + (tensor_place ^ t) * share
                for t in tensor_list
                for c in context_list
            ]
        )
        bases = jnp.take(block_order[0], starts // block_length) * block_length
        bases = bases + starts % block_length
        return (bases[:, None] + jnp.arange(share, dtype=jnp.int32)[None, :]).reshape(-1)

    key_places = chunk_places(range(context_count), range(tensor_count))
    query_places = chunk_places((0,), range(tensor_count))
    cosine_table, sine_table = rope_tables(wide(query_places))
    cosine_own, sine_own = cosine_table[:share], sine_table[:share]

    query_latent = low(norm_apply(latent[:, :QR], query_gain))
    keyval_latent = low(norm_apply(latent[:, QR : QR + KVR], keyval_gain))
    key_rope = low(rotate(latent[:, QR + KVR :], cosine_own, sine_own))
    key_rows = over_tensor(
        jnp.concatenate(collect(jnp.concatenate([keyval_latent, key_rope], axis=1)), axis=0)
    )
    query_rows = over_tensor(query_latent)
    keyval_rows = key_rows[:, :KVR]
    rope_rows = key_rows[:, KVR:]

    query_pre = product("lr,re->le", query_rows, query_full).reshape(
        local_length, local_heads, NOPE + ROPE
    )
    queries = low(
        jnp.concatenate(
            [
                query_pre[..., :NOPE],
                rotate(query_pre[..., NOPE:], cosine_table[:, None, :], sine_table[:, None, :]),
            ],
            axis=-1,
        )
    )
    keyval = low(product("lr,re->le", keyval_rows, keyval_full)).reshape(
        full_length, local_heads, NOPE + VDIM
    )
    key_nope = keyval[..., :NOPE]
    value_rows = keyval[..., NOPE:]
    visible = key_places[None, None, :] <= query_places[None, :, None]

    def score_table():
        raw_scores = product("ihd,jhd->hij", queries[..., :NOPE], key_nope)
        raw_scores = raw_scores + product("ihd,jd->hij", queries[..., NOPE:], rope_rows)
        return jnp.where(visible, raw_scores * score_scale, -1e30)

    scores = score_table()
    row_max = jnp.max(scores, axis=-1, keepdims=True)
    exponent = jnp.exp(scores - row_max)
    row_sum = jnp.sum(exponent, axis=-1, keepdims=True)
    probs_low = low(exponent / row_sum)
    attended = low(product("hij,jhd->ihd", probs_low, value_rows)).reshape(
        local_length, local_heads * VDIM
    )
    branch = sum_tensor(product("yz,hz->yh", attended, output_full))
    hidden = inputs + residual_scale * branch
    normed_feed = low(norm_apply(hidden, feed_gain))

    def spread(values):
        near = collect(values)
        far = [swap_far(item) for item in near]
        return jnp.concatenate(near + far, axis=0)

    def fold(values):
        count = share * context_count
        far = [
            wide(swap_far(low(values[count + i * share : count + (i + 1) * share])))
            for i in range(context_count)
        ]
        return give_back(
            [wide(values[i * share : (i + 1) * share]) + far[i] for i in range(context_count)]
        )

    unit_count = gate_weight.shape[1]
    unit_step = unit_count // context_count // 128 * 128
    unit_width = unit_count - unit_step * (context_count - 1)

    def fetch_units(shard):
        windows = jnp.stack(
            [shard[:, i * unit_step : i * unit_step + unit_width] for i in range(context_count)]
        )
        own = exchange(windows).reshape(-1, unit_width)
        own = jnp.concatenate([own, swap_fsdp(own)], axis=0)
        return (own, swap_near(own))

    unit_limit = jnp.where(context_place == context_count - 1, unit_width, unit_step)
    unit_mask = jnp.arange(unit_width)[None, :] < unit_limit
    gate_pair = fetch_units(gate_weight)
    up_pair = fetch_units(up_weight)
    down_pair = fetch_units(down_weight)

    incoming = own_first(
        wide(lax.dynamic_slice_in_dim(cotangent[0], tensor_place * share, share, 0))
    )
    seed_rows = spread(low(residual_scale * incoming))
    feed_rows = spread(normed_feed)

    out_part = 0.0
    back_part = 0.0
    weight_parts = []
    for gate_own, up_own, down_own in zip(gate_pair, up_pair, down_pair):
        gate = product("wt,tu->wu", feed_rows, gate_own)
        upward = product("wt,tu->wu", feed_rows, up_own)
        sigmoid_gate = jax.nn.sigmoid(gate)
        silu_gate = jnp.where(unit_mask, gate * sigmoid_gate, 0.0)
        activated = low(silu_gate * upward)
        act_grad = jnp.where(unit_mask, product("wt,tu->wu", seed_rows, down_own), 0.0)
        gate_grad = low(act_grad * upward * sigmoid_gate * (1.0 + gate * (1.0 - sigmoid_gate)))
        upward_grad = low(act_grad * silu_gate)
        out_part = out_part + product("mw,vw->mv", activated, down_own)
        back_part = back_part + product("mw,vw->mv", gate_grad, gate_own)
        back_part = back_part + product("mw,vw->mv", upward_grad, up_own)
        weight_parts.append(
            (
                product("bn,bt->nt", feed_rows, gate_grad),
                product("bn,bt->nt", feed_rows, upward_grad),
                product("bn,bt->nt", seed_rows, activated),
            )
        )

    normed_back = fold(back_part)
    feed_total = fold(out_part)
    output_rows = own_first(hidden + residual_scale * feed_total)

    def join_units(own, other):
        total = own + wide(swap_near(low(other)))
        total = low(total[:half] + wide(swap_fsdp(low(total[half:]))))
        return total.reshape(context_count, row_piece, unit_width)

    def close_units(got):
        got = wide(got)
        return jnp.concatenate(
            [got[i][:, :unit_step] for i in range(context_count - 1)] + [got[-1]], axis=1
        )

    down_total = join_units(weight_parts[0][2], weight_parts[1][2])
    gate_total = join_units(weight_parts[0][0], weight_parts[1][0])
    up_total = join_units(weight_parts[0][1], weight_parts[1][1])

    def sum_rows(own, other):
        total = own + wide(swap_fsdp(low(other)))
        got = exchange(low(total).reshape((context_count, -1) + own.shape[1:]))
        return jnp.sum(wide(got), axis=0)

    hidden_back, feed_gain_rows = norm_back(hidden, feed_gain, normed_back)
    hidden_grad = incoming + hidden_back
    branch_grad = over_tensor(low(residual_scale * hidden_grad))
    branch_grad, down_total, gate_total = lax.optimization_barrier(
        (branch_grad, down_total, gate_total)
    )
    down_got, gate_got, up_got = exchange(down_total), exchange(gate_total), exchange(up_total)
    attended_grad = low(product("nq,qk->nk", branch_grad, output_full)).reshape(
        local_length, local_heads, VDIM
    )
    output_part = product("xg,xn->gn", branch_grad, attended)

    scores = score_table()
    attend_probs = jnp.exp(scores - row_max) / row_sum
    probs_low = low(attend_probs)
    prob_grad = product("ihd,jhd->hij", attended_grad, value_rows)
    score_grad = low(
        attend_probs * (prob_grad - jnp.sum(attend_probs * prob_grad, axis=-1, keepdims=True))
    )
    score_grad, down_got = lax.optimization_barrier((score_grad, down_got))
    query_grad = (
        jnp.concatenate(
            [
                product("hij,jhd->ihd", score_grad, key_nope),
                product("hij,jd->ihd", score_grad, rope_rows),
            ],
            axis=-1,
        )
        * score_scale
    )
    key_nope_grad = product("hij,ihd->jhd", score_grad, queries[..., :NOPE]) * score_scale
    value_grad = product("hij,ihd->jhd", probs_low, attended_grad)
    rope_grad = product("hij,ihd->jd", score_grad, queries[..., NOPE:]) * score_scale
    keyval_grad = low(jnp.concatenate([key_nope_grad, value_grad], axis=-1)).reshape(
        full_length, local_heads * (NOPE + VDIM)
    )
    key_back = jnp.concatenate(
        [product("le,re->lr", keyval_grad, keyval_full), rope_grad], axis=1
    )
    key_back, gate_got = lax.optimization_barrier((key_back, gate_got))
    count = full_length // 2
    key_back = key_back[:count] + wide(swap_far(low(key_back[count:])))
    count = count // 2
    key_back = key_back[:count] + wide(swap_near(low(key_back[count:])))
    key_back = give_back([key_back[i * share : (i + 1) * share] for i in range(context_count)])

    query_pre_grad = low(
        jnp.concatenate(
            [
                query_grad[..., :NOPE],
                rotate_back(
                    query_grad[..., NOPE:], cosine_table[:, None, :], sine_table[:, None, :]
                ),
            ],
            axis=-1,
        ).reshape(local_length, local_heads * (NOPE + ROPE))
    )
    query_back = sum_tensor(product("le,re->lr", query_pre_grad, query_full))
    query_part = product("lr,le->re", query_rows, query_pre_grad)
    keyval_part = product("lr,le->re", keyval_rows, keyval_grad)

    query_back, up_got = lax.optimization_barrier((query_back, up_got))
    output_sum = sum_rows(output_part[:half], output_part[half:])
    query_lat_grad, query_gain_rows = norm_back(latent[:, :QR], query_gain, query_back)
    keyval_lat_grad, keyval_gain_rows = norm_back(
        latent[:, QR : QR + KVR], keyval_gain, key_back[:, :KVR]
    )
    rope_lat_grad = rotate_back(key_back[:, KVR:], cosine_own, sine_own)
    latent_grad = jnp.concatenate([query_lat_grad, keyval_lat_grad, rope_lat_grad], axis=-1)
    latent_grad_rows = jnp.concatenate(collect(low(latent_grad * input_inverse)), axis=0)
    latent_sum_part = product("po,pm->om", scaled_rows, latent_grad_rows)
    normed_grad_part = low(product("cj,kj->ck", latent_grad_rows, latent_pair)).reshape(
        context_count, share, shard_count * row_piece
    )
    returned = jnp.stack(
        [normed_grad_part[0]] + [shift(normed_grad_part[step], -step) for step in others]
    )
    normed_grad = jnp.stack(
        [
            lax.dynamic_index_in_dim(returned, (i - context_place) % context_count, 0, False)
            for i in range(context_count)
        ]
    )
    normed_grad = (
        wide(normed_grad)
        .reshape(context_count, share, shard_count, row_piece)
        .transpose(1, 2, 0, 3)
        .reshape(share, width)
        / input_inverse
    )
    normed_grad, output_sum = lax.optimization_barrier((normed_grad, output_sum))
    input_back, attend_gain_rows = norm_back(inputs, attend_gain, normed_grad)
    input_grad = own_first(hidden_grad + input_back)

    gain_sum = jnp.concatenate(
        [
            own_first(jnp.sum(attend_gain_rows, axis=0)),
            jnp.sum(query_gain_rows, axis=0),
            jnp.sum(keyval_gain_rows, axis=0),
            own_first(jnp.sum(feed_gain_rows, axis=0)),
        ]
    )
    gain_sum = gain_sum.reshape(owner_count, -1)
    gain_sum = gain_sum + swap_near(gain_sum)
    gain_sum = gain_sum + swap_far(gain_sum)
    gain_sum = jnp.sum(
        lax.all_to_all(gain_sum, (FSDP, CTX), split_axis=0, concat_axis=0), axis=0
    )

    latent_sum = low(
        latent_sum_part[:row_piece] + wide(swap_fsdp(low(latent_sum_part[row_piece:])))
    )
    latent_sum = low(wide(latent_sum) + wide(swap_near(latent_sum)))
    latent_sum = wide(latent_sum) + wide(swap_far(latent_sum))

    def halves(values):
        stacked = values.reshape((shard_count, -1) + values.shape[1:])
        return (
            lax.dynamic_index_in_dim(stacked, shard_place, 0, False),
            lax.dynamic_index_in_dim(stacked, 1 - shard_place, 0, False),
        )

    summed = (
        latent_sum,
        sum_rows(*halves(query_part)),
        sum_rows(*halves(keyval_part)),
        output_sum,
        close_units(gate_got),
        close_units(up_got),
        close_units(down_got),
        gain_sum,
    )
    shards = tuple(item / token_total for item in summed)
    lead_flag = wide(tensor_place == 0)
    local_square = lead_flag * (jnp.sum(shards[0] * shards[0]) + jnp.sum(shards[7] * shards[7]))
    for shard_grad in shards[1:7]:
        local_square = local_square + jnp.sum(shard_grad * shard_grad)
    square = jnp.full((8, 128), local_square)
    square = square + swap_near(square)
    square = square + swap_far(square)
    square = square + swap_fsdp(square)
    around = [shift(square, step) for step in others]
    square = (square + around[1]) + (around[0] + around[2])
    grad_norm = jnp.sqrt(square[0, 0])
    factor = clip_level / jnp.maximum(grad_norm, clip_level)
    stepped = [
        adam_step(
            weights_local[i], shards[i], firsts[i], seconds[i], factor, i < 7
        )
        for i in range(8)
    ]
    return (
        (output_rows[None], input_grad[None])
        + shards
        + (grad_norm,)
        + tuple(item[0] for item in stepped)
        + tuple(item[1] for item in stepped)
        + tuple(item[2] for item in stepped)
    )


def solution(mesh):
    sizes = dict(mesh.shape)
    planes = sizes[FSDP] == 2 and sizes[CTX] == 4 and sizes[TP] == 4
    body = body_planes if planes else body_gathered
    placed = (
        P(FSDP, CTX, None),
        P(FSDP, CTX, None),
        P(FSDP, None),
        ROWS,
        SPLIT,
        SPLIT,
        SPLIT,
        SPLIT,
        SPLIT,
        SPLIT,
        GAIN,
        ROWS,
        SPLIT,
        SPLIT,
        SPLIT,
        SPLIT,
        SPLIT,
        SPLIT,
        GAIN,
        ROWS,
        SPLIT,
        SPLIT,
        SPLIT,
        SPLIT,
        SPLIT,
        SPLIT,
        GAIN,
    )
    return jax.shard_map(
        body,
        mesh=mesh,
        in_specs=placed,
        out_specs=(
            P(FSDP, (CTX, TP), None),
            P(FSDP, (CTX, TP), None),
            ROWS,
            SPLIT,
            SPLIT,
            SPLIT,
            SPLIT,
            SPLIT,
            SPLIT,
            GAIN,
            P(),
            ROWS,
            SPLIT,
            SPLIT,
            SPLIT,
            SPLIT,
            SPLIT,
            SPLIT,
            GAIN,
            ROWS,
            SPLIT,
            SPLIT,
            SPLIT,
            SPLIT,
            SPLIT,
            SPLIT,
            GAIN,
            ROWS,
            SPLIT,
            SPLIT,
            SPLIT,
            SPLIT,
            SPLIT,
            SPLIT,
            GAIN,
        ),
        check_vma=False,
    )
```
